32 devices in a mesh: shard: 8 (over z, x), seq: 4 (over y, core).
Axes of the slice: x: 2, y: 2, z: 4, core: 2. Of those that a mesh axis runs over, the one named last changes fastest.
Arguments:
- clips: bfloat16 [8, 1568, 1024], P('shard', 'seq'), may hold values from -6 to 6
- clip_mask: int32 [8], P('shard'), may hold values 0 or 1
- norm1_gain: float32 [1024], P(('shard', 'seq')), may hold values from 0.1 to 1.9
- norm1_shift: float32 [1024], P(('shard', 'seq')), may hold values from -3 to 3
- query_weight: float32 [1024, 1024], P(('shard', 'seq')), may hold values from -0.1875 to 0.1875
- query_bias: float32 [1024], P(('shard', 'seq')), may hold values from -3 to 3
- key_weight: float32 [1024, 1024], P(('shard', 'seq')), may hold values from -0.1875 to 0.1875
- value_weight: float32 [1024, 1024], P(('shard', 'seq')), may hold values from -0.1875 to 0.1875
- value_bias: float32 [1024], P(('shard', 'seq')), may hold values from -0.3 to 0.3
- out_weight: float32 [1024, 1024], P(('shard', 'seq')), may hold values from -4 to 4
- out_bias: float32 [1024], P(('shard', 'seq')), may hold values from -1.2 to 1.2
- norm2_gain: float32 [1024], P(('shard', 'seq')), may hold values from 0.1 to 1.9
- norm2_shift: float32 [1024], P(('shard', 'seq')), may hold values from -3 to 3
- fc1_weight: float32 [1024, 4096], P(('shard', 'seq')), may hold values from -0.1875 to 0.1875
- fc1_bias: float32 [4096], P(('shard', 'seq')), may hold values from -3 to 3
- fc2_weight: float32 [4096, 1024], P(('shard', 'seq')), may hold values from -0.09375 to 0.09375
- fc2_bias: float32 [1024], P(('shard', 'seq')), may hold values from -1.2 to 1.2
- cotangent: bfloat16 [8, 1568, 1024], P('shard', 'seq'), may hold values from -6 to 6
Outputs:
- layer_out: bfloat16 [8, 1568, 1024], P('shard', 'seq')
- grad_clips: bfloat16 [8, 1568, 1024], P('shard', 'seq')
- grad_norm1_gain: float32 [1024], P(('shard', 'seq'))
- grad_norm1_shift: float32 [1024], P(('shard', 'seq'))
- grad_query_weight: float32 [1024, 1024], P(('shard', 'seq'))
- grad_query_bias: float32 [1024], P(('shard', 'seq'))
- grad_key_weight: float32 [1024, 1024], P(('shard', 'seq'))
- grad_value_weight: float32 [1024, 1024], P(('shard', 'seq'))
- grad_value_bias: float32 [1024], P(('shard', 'seq'))
- grad_out_weight: float32 [1024, 1024], P(('shard', 'seq'))
- grad_out_bias: float32 [1024], P(('shard', 'seq'))
- grad_norm2_gain: float32 [1024], P(('shard', 'seq'))
- grad_norm2_shift: float32 [1024], P(('shard', 'seq'))
- grad_fc1_weight: float32 [1024, 4096], P(('shard', 'seq'))
- grad_fc1_bias: float32 [4096], P(('shard', 'seq'))
- grad_fc2_weight: float32 [4096, 1024], P(('shard', 'seq'))
- grad_fc2_bias: float32 [1024], P(('shard', 'seq'))
The draws below stay inside these ranges and needn't reach their ends.
All inputs are finite; a program needn't handle non-finite values. No bound on the sum of `clip_mask` on one device may be relied on, other than what follows from the above.
Results may differ from the reference program's by a relative error of at most 0.012.
The reference program's roundings to bfloat16 on the way count: a program that leaves them out, or rounds other values in their place, can miss the bound.
Values may be sent and summed in bfloat16 or wider, within the bound.
A program may use at most 192 MiB of HBM per device.

```python
import jax
import jax.numpy as jnp
from jax import lax

D = 1024
HEADS = 16
HEAD_DIM = 64
FF = 4096
LENGTH = 1568
CLIPS = 8


def plant(array, own_key, smallest, high):
    longest = array.shape.index(max(array.shape))
    spots = []
    for shift in (0, 1):
        where = [jax.random.randint(jax.random.fold_in(own_key, axis), (), 0, length) for axis, length in enumerate(array.shape)]
        where[longest] = (where[longest] + shift) % array.shape[longest]
        spots.append(tuple(where))
    return array.at[spots[0]].set(smallest).at[spots[1]].set(high)


def with_spikes(values, stream_key, source, target, parts, factor):
    owner, partner = [(jnp.arange(values.shape[axis_at]) // (values.shape[axis_at] // parts)).reshape([-1 if axis == axis_at else 1 for axis in range(values.ndim)]) for axis_at in (source, target)]
    chosen = jax.random.permutation(stream_key, parts)[partner]
    strong = (owner == chosen) | (owner == (partner + parts // 2) % parts)
    return jnp.where(strong, factor * values, values)


def steps_of(key, extent, split, low, high):
    level, own = 1.0, jax.random.fold_in(key, 6)
    for axis_at, blocks in split:
        draws = jnp.exp(jax.random.uniform(jax.random.fold_in(own, axis_at), (blocks,), jnp.float32, low / len(split), high / len(split)))
        level = level * jnp.repeat(draws, extent[axis_at] // blocks).reshape([-1 if axis == axis_at else 1 for axis in range(len(extent))])
    return level


def noise(rng, shape, spread, reach, cuts=(), held_as=jnp.bfloat16):
    loudness = steps_of(rng, shape, cuts, -0.22, 0.18) if cuts else 1.0
    values = jax.random.normal(rng, shape, jnp.float32) * spread * loudness
    return jnp.minimum(jnp.maximum(values, -reach), reach).astype(held_as)


def bell_draw_with(own_key, dims, width, bound, cuts, heavy, kind=jnp.bfloat16):
    entries = width * jax.random.normal(own_key, dims, jnp.float32)
    if cuts:
        entries = entries * steps_of(own_key, dims, cuts, -0.22, 0.18)
    return jnp.clip(with_spikes(entries, jax.random.fold_in(own_key, 3), *heavy), -bound, bound).astype(kind)


def setup_inputs(seed: int = 0) -> dict:
    splits = jax.random.split(jax.random.key(seed), 19)
    return {
        "clips": noise(splits[0], (CLIPS, LENGTH, D), 1.0, 6.0, ((0, 8), (1, 4))),
        "clip_mask": plant((jax.random.randint(splits[1], (CLIPS,), 0, 4) < 3).astype(jnp.int32), jax.random.fold_in(splits[1], 1), 0, 1),
        "norm1_gain": jnp.clip(1.0 + 0.18 * jax.random.normal(splits[2], (D,), jnp.float32), 0.1, 1.9),
        "norm1_shift": noise(splits[3], (D,), 0.5, 3.0, ((0, 32),), jnp.float32),
        "query_weight": noise(splits[4], (D, D), D ** -0.5, 0.1875, ((0, 32),), jnp.float32),
        "query_bias": noise(splits[5], (D,), 0.5, 3.0, ((0, 32),), jnp.float32),
        "key_weight": noise(splits[6], (D, D), D ** -0.5, 0.1875, ((0, 32),), jnp.float32),
        "value_weight": noise(splits[7], (D, D), D ** -0.5, 0.1875, ((0, 32),), jnp.float32),
        "value_bias": noise(splits[8], (D,), 0.05, 0.3, ((0, 32),), jnp.float32),
        "out_weight": noise(splits[9], (D, D), (max(D * 4 // LENGTH, 1)) ** -0.5, 4.0, ((0, 32),), jnp.float32),
        "out_bias": noise(splits[10], (D,), 0.2, 1.2, ((0, 32),), jnp.float32),
        "norm2_gain": jnp.clip(1.0 + 0.18 * jax.random.normal(splits[11], (D,), jnp.float32), 0.1, 1.9),
        "norm2_shift": noise(splits[12], (D,), 0.5, 3.0, ((0, 32),), jnp.float32),
        "fc1_weight": noise(splits[13], (D, FF), D ** -0.5, 0.1875, ((0, 32),), jnp.float32),
        "fc1_bias": noise(splits[14], (FF,), 0.5, 3.0, ((0, 32),), jnp.float32),
        "fc2_weight": noise(splits[15], (FF, D), FF ** -0.5, 0.09375, ((0, 32),), jnp.float32),
        "fc2_bias": noise(splits[16], (D,), 0.2, 1.2, ((0, 32),), jnp.float32),
        "cotangent": bell_draw_with(splits[17], (CLIPS, LENGTH, D), 1.0, 6.0, ((0, 8), (1, 4)), (0, 2, 8, 2.0)),
    }


EPSILON = 1e-06

@jax.custom_vjp
def low(v):
    return lax.optimization_barrier(v.astype(jnp.bfloat16)).astype(jnp.float32)

@jax.custom_vjp
def low_back(v):
    return v

def low_keep(v):
    return (low(v), None)

def low_pass(kept, grad):
    return (grad,)

def back_keep(v):
    return (v, None)

def back_low(kept, grad):
    return (low(grad),)
low.defvjp(low_keep, low_pass)
low_back.defvjp(back_keep, back_low)

def product(left, right):
    return jnp.dot(left, right, precision=lax.Precision.HIGHEST, preferred_element_type=jnp.float32)

def layer_norm(values, gain, shift):
    average = lax.optimization_barrier(jnp.mean(values, -1, keepdims=True))
    centred = values - average
    variance = lax.optimization_barrier(jnp.mean(centred * centred, -1, keepdims=True))
    return centred * lax.rsqrt(variance + EPSILON) * gain + shift

def clip_layer(clip, params):
    gain_first, shift_first, query_matrix, query_offset, key_matrix, value_matrix, value_offset, output_matrix, output_offset, gain_second, shift_second, expand_matrix, expand_offset, reduce_matrix, reduce_offset = params
    length = clip.shape[0]
    hidden_one = low(layer_norm(clip, gain_first, shift_first))
    query = low(low_back(product(hidden_one, query_matrix) + query_offset))
    keys = low(low_back(product(hidden_one, key_matrix)))
    values = low(low_back(product(hidden_one, value_matrix) + value_offset))
    query_heads = query.reshape(length, HEADS, HEAD_DIM)
    key_heads = keys.reshape(length, HEADS, HEAD_DIM)
    value_heads = values.reshape(length, HEADS, HEAD_DIM)
    scores = jnp.einsum('qhd,khd->hqk', query_heads, key_heads, precision=lax.Precision.HIGHEST)
    scores = low_back(scores * HEAD_DIM ** (-0.5))
    raised = jnp.exp(scores - lax.optimization_barrier(jnp.max(scores, -1, keepdims=True)))
    probs = low(raised / lax.optimization_barrier(jnp.sum(raised, -1, keepdims=True)))
    mixed = jnp.einsum('hqk,khd->qhd', probs, value_heads, precision=lax.Precision.HIGHEST)
    mixed = low(low_back(mixed.reshape(length, HEADS * HEAD_DIM)))
    middle = clip + low_back(product(mixed, output_matrix) + output_offset)
    hidden_two = low(layer_norm(middle, gain_second, shift_second))
    inner = low_back(product(hidden_two, expand_matrix) + expand_offset)
    active = low(jax.nn.gelu(inner, approximate=False))
    return middle + low_back(product(active, reduce_matrix) + reduce_offset)

def reference(clips, clip_mask, norm1_gain, norm1_shift, query_weight, query_bias, key_weight, value_weight, value_bias, out_weight, out_bias, norm2_gain, norm2_shift, fc1_weight, fc1_bias, fc2_weight, fc2_bias, cotangent):
    masters = (norm1_gain, norm1_shift, query_weight, query_bias, key_weight, value_weight, value_bias, out_weight, out_bias, norm2_gain, norm2_shift, fc1_weight, fc1_bias, fc2_weight, fc2_bias)
    weight_mask = clip_mask.astype(jnp.float32)[:, None, None]

    def forward(inputs, params):
        lowered = tuple((low(piece) for piece in params))
        layer = jax.checkpoint(lambda clip: clip_layer(clip, lowered))
        return lax.map(layer, inputs) * weight_mask
    result, pullback = jax.vjp(forward, clips.astype(jnp.float32), masters)
    grad_inputs, grad_params = pullback(cotangent.astype(jnp.float32))
    return (result.astype(jnp.bfloat16), grad_inputs.astype(jnp.bfloat16), grad_params[0], grad_params[1], grad_params[2], grad_params[3], grad_params[4], grad_params[5], grad_params[6], grad_params[7], grad_params[8], grad_params[9], grad_params[10], grad_params[11], grad_params[12], grad_params[13], grad_params[14])
```

```python
import jax
import jax.numpy as jnp
from jax import lax
from jax.sharding import PartitionSpec as P

HEAD_DIM = 64


EPSILON = 1e-06


def for_sending(value):
    return jax.tree.map(lambda a: a.astype(jnp.bfloat16) if a.dtype == jnp.float32 else a, value)


def matmul(left, right):
    return jnp.dot(left, right, preferred_element_type=jnp.float32)


def matmul_right_t(left, right):
    return lax.dot_general(
        left, right, (((1,), (1,)), ((), ())), preferred_element_type=jnp.float32
    )


def matmul_left_t(left, right):
    return lax.dot_general(
        left, right, (((0,), (0,)), ((), ())), preferred_element_type=jnp.float32
    )


def gelu_exact(values):
    return jax.nn.gelu(values, approximate=False)


def normalize(values):
    average = jnp.mean(values, -1, keepdims=True)
    centred = values - average
    variance = jnp.mean(centred * centred, -1, keepdims=True)
    inverse = lax.rsqrt(variance + EPSILON)
    return (centred * inverse, inverse)


def norm_back(grad_normed, normed, inverse, gain):
    grad_gain = jnp.sum(grad_normed * normed, 0)
    grad_shift = jnp.sum(grad_normed, 0)
    scaled = grad_normed * gain
    plain_mean = jnp.mean(scaled, -1, keepdims=True)
    cross_mean = jnp.mean(scaled * normed, -1, keepdims=True)
    return (grad_gain, grad_shift, inverse * (scaled - plain_mean - normed * cross_mean))


def attend_clip(inputs):
    query, keys, values = inputs
    length = query.shape[0]
    heads = query.shape[1] // HEAD_DIM
    scale = HEAD_DIM ** (-0.5)
    query = query.reshape(length, heads, HEAD_DIM)
    keys = keys.reshape(length, heads, HEAD_DIM)
    values = values.reshape(length, heads, HEAD_DIM)
    half = length // 2
    outputs = []
    totals = []
    for block in range(2):
        rows_query = query[block * half : (block + 1) * half]
        scores = (
            jnp.einsum("qhd,khd->hqk", rows_query, keys, preferred_element_type=jnp.float32) * scale
        )
        row_max = jnp.max(scores, -1, keepdims=True)
        raised = jnp.exp(scores - row_max)
        summed = jnp.sum(raised, -1, keepdims=True)
        probs = (raised / summed).astype(jnp.bfloat16)
        mixed = jnp.einsum("hqk,khd->qhd", probs, values, preferred_element_type=jnp.float32)
        outputs.append(mixed.astype(jnp.bfloat16))
        totals.append((row_max + jnp.log(summed))[..., 0])
    joined = jnp.concatenate(outputs, 0).reshape(length, heads * HEAD_DIM)
    return (joined, jnp.concatenate(totals, 1))


def attend_back(inputs):
    query, keys, values, totals, grad_out = inputs
    length = query.shape[0]
    heads = query.shape[1] // HEAD_DIM
    scale = HEAD_DIM ** (-0.5)
    query = query.reshape(length, heads, HEAD_DIM)
    keys = keys.reshape(length, heads, HEAD_DIM)
    values = values.reshape(length, heads, HEAD_DIM)
    grad_out = grad_out.reshape(length, heads, HEAD_DIM)
    half = length // 2
    grad_keys = jnp.zeros((length, heads, HEAD_DIM), jnp.float32)
    grad_values = jnp.zeros((length, heads, HEAD_DIM), jnp.float32)
    query_parts = []
    for block in range(2):
        rows_query = query[block * half : (block + 1) * half]
        rows_grad = grad_out[block * half : (block + 1) * half]
        scores = (
            jnp.einsum("qhd,khd->hqk", rows_query, keys, preferred_element_type=jnp.float32) * scale
        )
        probs = jnp.exp(scores - totals[:, block * half : (block + 1) * half, None])
        grad_probs = jnp.einsum(
            "qhd,khd->hqk", rows_grad, values, preferred_element_type=jnp.float32
        )
        weighted = jnp.sum(probs * grad_probs, -1, keepdims=True)
        grad_scores = (probs * (grad_probs - weighted)).astype(jnp.bfloat16)
        part = (
            jnp.einsum("hqk,khd->qhd", grad_scores, keys, preferred_element_type=jnp.float32)
            * scale
        )
        query_parts.append(part.astype(jnp.bfloat16))
        grad_keys = (
            grad_keys
            + jnp.einsum(
                "hqk,qhd->khd", grad_scores, rows_query, preferred_element_type=jnp.float32
            )
            * scale
        )
        grad_values = grad_values + jnp.einsum(
            "hqk,qhd->khd",
            probs.astype(jnp.bfloat16),
            rows_grad,
            preferred_element_type=jnp.float32,
        )
    width = heads * HEAD_DIM
    grad_query = jnp.concatenate(query_parts, 0).reshape(length, width)
    return (
        grad_query,
        grad_keys.astype(jnp.bfloat16).reshape(length, width),
        grad_values.astype(jnp.bfloat16).reshape(length, width),
    )


def tensor_parallel(shards, seqs):
    axes = ("shard", "seq")

    def run(
        clips, clip_mask, norm1_gain, norm1_shift, query_weight, query_bias, key_weight,
        value_weight, value_bias, out_weight, out_bias, norm2_gain, norm2_shift, fc1_weight,
        fc1_bias, fc2_weight, fc2_bias, cotangent,
    ):
        low = jnp.bfloat16
        wide = jnp.float32
        _, local, width = clips.shape
        rows = query_weight.shape[0]
        hidden_rows, hidden_local = fc2_weight.shape[0], fc1_weight.shape[1] // seqs
        part = width // seqs
        heads = part // HEAD_DIM
        length = local * seqs
        place = lax.axis_index("seq")
        projections = jnp.stack([query_weight, key_weight, value_weight], 1).astype(low)
        projections = projections.reshape(rows, 3, seqs, part).transpose(2, 0, 1, 3)
        expand = fc1_weight.astype(low).reshape(rows, shards, seqs, hidden_rows)
        expand = expand.transpose(2, 0, 1, 3)
        outward = jnp.concatenate(
            [projections.reshape(seqs, rows, 3 * part), expand.reshape(seqs, rows, hidden_local)], -1
        )
        inward = lax.all_to_all(outward, "seq", 0, 0, tiled=True).reshape(seqs * rows, -1)
        packed = lax.all_gather(inward, "shard", axis=0, tiled=True)
        projection, expand_matrix = packed[:, : 3 * part], packed[:, 3 * part :]
        reduce_matrix = lax.all_gather(fc2_weight.astype(low), "shard", axis=0, tiled=True)
        output_matrix = lax.all_gather(out_weight.astype(low), axes, axis=0, tiled=True)
        small = jnp.stack(
            [norm1_gain, norm1_shift, query_bias, value_bias, out_bias, norm2_gain, norm2_shift, fc2_bias]
        ).astype(low)
        small = lax.all_gather(small, axes, axis=1, tiled=True).astype(wide)
        gain_one, shift_one, bias_q, bias_v, bias_o, gain_two, shift_two, bias_r = small
        bias_e = lax.all_gather(fc1_bias.astype(low), "shard", axis=0, tiled=True).astype(wide)

        inputs = clips[0].astype(wide)
        normed_one, inverse_one = normalize(inputs)
        hidden_one = (normed_one * gain_one + shift_one).astype(low)
        hidden_one = lax.all_gather(hidden_one, "seq", axis=0, tiled=True)
        own = lambda vector: lax.dynamic_slice(vector, (place * part,), (part,))
        bias = jnp.concatenate([own(bias_q), jnp.zeros((part,), wide), own(bias_v)])
        qkv = (matmul(hidden_one, projection) + bias).astype(low)
        query, keys, values = qkv[:, :part], qkv[:, part : 2 * part], qkv[:, 2 * part :]
        mixed_heads, totals = attend_clip((query, keys, values))
        mixed = lax.all_to_all(mixed_heads, "seq", 0, 1, tiled=True)
        middle = inputs + matmul(mixed, output_matrix) + bias_o
        normed_two, inverse_two = normalize(middle)
        hidden_two = (normed_two * gain_two + shift_two).astype(low)
        hidden_two = lax.all_gather(hidden_two, "seq", axis=0, tiled=True)

        mask = clip_mask[0].astype(wide)
        grad_result = cotangent[0].astype(wide) * mask
        grad_last = grad_result.astype(low)
        grad_reduce_bias = jnp.sum(grad_last.astype(wide), 0)
        grad_last = lax.all_gather(grad_last, "seq", axis=0, tiled=True)
        inner = matmul(hidden_two, expand_matrix) + bias_e
        active_float, pullback = jax.vjp(gelu_exact, inner)
        active = active_float.astype(low)
        result = lax.psum_scatter(
            matmul(active, reduce_matrix).astype(low), "seq", scatter_dimension=0, tiled=True
        )
        layer_out = ((middle + result.astype(wide) + bias_r) * mask).astype(low)[None]
        grad_reduce = matmul_left_t(active, grad_last)
        grad_inner = pullback(matmul_right_t(grad_last, reduce_matrix))[0].astype(low)
        grad_expand_bias = jnp.sum(grad_inner.astype(wide), 0)
        grad_expand = matmul_left_t(hidden_two, grad_inner)
        grad_hidden_two = lax.psum_scatter(
            matmul_right_t(grad_inner, expand_matrix).astype(low), "seq", scatter_dimension=0, tiled=True
        ).astype(wide)
        grad_gain_two, grad_shift_two, grad_through = norm_back(
            grad_hidden_two, normed_two, inverse_two, gain_two
        )
        grad_middle = grad_result + grad_through
        grad_branch = grad_middle.astype(low)
        grad_output_bias = jnp.sum(grad_branch.astype(wide), 0)
        grad_output = matmul_left_t(mixed, grad_branch)
        grad_mixed = matmul_right_t(grad_branch, output_matrix).astype(low)
        grad_mixed = lax.all_to_all(grad_mixed, "seq", 1, 0, tiled=True)

        grads = attend_back((query, keys, values, totals, grad_mixed))
        grad_qkv = jnp.concatenate(grads, 1)
        grad_projection = matmul_left_t(hidden_one, grad_qkv)
        grad_bias = jnp.sum(grad_qkv.astype(wide), 0)
        grad_hidden_one = lax.psum_scatter(
            matmul_right_t(grad_qkv, projection).astype(low), "seq", scatter_dimension=0, tiled=True
        ).astype(wide)
        grad_gain_one, grad_shift_one, grad_entry = norm_back(
            grad_hidden_one, normed_one, inverse_one, gain_one
        )
        grad_clips = (grad_middle + grad_entry).astype(low)[None]

        spread = lambda v: lax.dynamic_update_slice(jnp.zeros((width,), wide), v, (place * part,))
        small = jnp.stack(
            [
                grad_gain_one, grad_shift_one, spread(grad_bias[:part]), spread(grad_bias[2 * part :]),
                grad_output_bias, grad_gain_two, grad_shift_two, grad_reduce_bias,
            ]
        )
        small = lax.psum_scatter(small, axes, scatter_dimension=1, tiled=True)
        grad_expand_bias = lax.psum_scatter(grad_expand_bias, "shard", scatter_dimension=0, tiled=True)
        packed = jnp.concatenate([grad_projection, grad_expand], 1).astype(low)
        packed = lax.psum_scatter(packed, "shard", scatter_dimension=0, tiled=True)
        packed = lax.all_to_all(packed.reshape(seqs, rows, -1), "seq", 0, 0, tiled=True).astype(wide)
        grad_qkv_rows = packed[..., : 3 * part].reshape(seqs, rows, 3, part).transpose(2, 1, 0, 3)
        grad_qkv_rows = grad_qkv_rows.reshape(3, rows, width)
        grad_expand = packed[..., 3 * part :].reshape(seqs, rows, shards, hidden_rows)
        grad_expand = grad_expand.transpose(1, 2, 0, 3).reshape(rows, -1)
        grad_reduce = lax.psum_scatter(
            grad_reduce.astype(low), "shard", scatter_dimension=0, tiled=True
        ).astype(wide)
        grad_output = lax.psum_scatter(
            grad_output.astype(low), axes, scatter_dimension=0, tiled=True
        ).astype(wide)
        return (
            layer_out, grad_clips, small[0], small[1], grad_qkv_rows[0], small[2], grad_qkv_rows[1],
            grad_qkv_rows[2], small[3], grad_output, small[4], small[5], small[6], grad_expand,
            grad_expand_bias, grad_reduce, small[7],
        )

    return run


def solution(mesh):
    return jax.shard_map(
        tensor_parallel(mesh.shape["shard"], mesh.shape["seq"]),
        mesh=mesh,
        in_specs=(
            P("shard", "seq", None),
            P("shard"),
            P(("shard", "seq")),
            P(("shard", "seq")),
            P(("shard", "seq"), None),
            P(("shard", "seq")),
            P(("shard", "seq"), None),
            P(("shard", "seq"), None),
            P(("shard", "seq")),
            P(("shard", "seq"), None),
            P(("shard", "seq")),
            P(("shard", "seq")),
            P(("shard", "seq")),
            P(("shard", "seq"), None),
            P(("shard", "seq")),
            P(("shard", "seq"), None),
            P(("shard", "seq")),
            P("shard", "seq", None),
        ),
        out_specs=(
            P("shard", "seq", None),
            P("shard", "seq", None),
            P(("shard", "seq")),
            P(("shard", "seq")),
            P(("shard", "seq"), None),
            P(("shard", "seq")),
            P(("shard", "seq"), None),
            P(("shard", "seq"), None),
            P(("shard", "seq")),
            P(("shard", "seq"), None),
            P(("shard", "seq")),
            P(("shard", "seq")),
            P(("shard", "seq")),
            P(("shard", "seq"), None),
            P(("shard", "seq")),
            P(("shard", "seq"), None),
            P(("shard", "seq")),
        ),
        check_vma=False,
    )
```
